32 devices in a mesh: groups: 2 (over y), dp: 16 (over z, x, core).
Axes of the slice: x: 2, y: 2, z: 4, core: 2. Of those that a mesh axis runs over, the one named last changes fastest.
Arguments:
- layer_inputs: bfloat16 [2, 32, 1344, 512], P(None, ('groups', 'dp')), parts along dimension 1, may hold values from -6 to 6
- out_grads: bfloat16 [2, 32, 1344, 512], P(None, ('groups', 'dp')), parts along dimension 1, may hold values from -6 to 6
- error_prev: bfloat16 [2, 49152, 512], P(None, ('groups', 'dp')), parts along dimension 1, may hold values from -4 to 4
- q_start: float32 [2, 512, 64], replicated, may hold values from -0.25 to 0.25
Outputs:
- panels: float32 [4, 1536, 64], P('groups'), parts along dimension 0
- factors: float32 [4, 512, 64], P('groups'), parts along dimension 0
- error_next: bfloat16 [2, 49152, 512], P(None, ('groups', 'dp')), parts along dimension 1
The draws below stay inside these ranges and needn't reach their ends.
There are 2 independent parts, one for each index of `groups`. The reference program is written for one: setup_inputs(seed, part) draws one part's arguments, and reference() takes and returns one part's arrays. A program takes and returns all parts, laid end to end along the dimension named above; an argument that names none is the same for every part. Nothing has to cross between parts.
All inputs are finite; a program needn't handle non-finite values.
Results may differ from the reference program's by a relative error of at most 0.001.
Values sent between devices are 32-bit elements; how exact they have to be, the bound alone decides.
No kernel may reach another device: no remote copies, remote signals or barrier semaphores. Data moves between devices by JAX's collectives and lax.ppermute only.
A program may use at most 64 MiB of HBM per device.

```python
import math
import jax
import jax.numpy as jnp
from jax import lax

C = 512
RANK = 64
LEN = 1344
LAYERS = 2
DILATION = 64
SEQS = 16
ERR_ROWS = 24576
N_DP = 16


def block_levels(own_key, shape, split, smallest, high):
    gain = 1.0
    for dim, shards_of in split:
        steps = jax.random.uniform(jax.random.fold_in(jax.random.fold_in(own_key, 6), dim), (shards_of,), jnp.float32, smallest / len(split), high / len(split))
        gain = gain * jnp.repeat(jnp.exp(steps), shape[dim] // shards_of).reshape((-1,) + (1,) * (len(shape) - 1 - dim))
    return gain


def normal_values(rng, shape, scale, limit, split=(), held_as=jnp.bfloat16):
    result = scale * jax.random.normal(rng, shape, jnp.float32)
    if split:
        result = result * block_levels(rng, shape, split, -0.22, 0.18)
    return jnp.clip(result, -limit, limit).astype(held_as)


def setup_inputs(seed: int = 0, part: int = 0) -> dict:
    key_of = jax.random.split(jax.random.key(seed), 5)
    part_keys = jax.random.split(jax.random.fold_in(key_of[4], part), 5)
    layer_inputs = normal_values(part_keys[0], (LAYERS, SEQS, LEN, C), 1.0, 6.0, ((1, 16),))
    out_grads = normal_values(part_keys[1], (LAYERS, SEQS, LEN, C), 1.0, 6.0, ((1, 16),))
    error_prev = normal_values(part_keys[2], (LAYERS, ERR_ROWS, C), 0.5, 4.0, ((1, 16),))
    q_start = normal_values(key_of[3], (LAYERS, C, RANK), C ** -0.5, 0.25, (), jnp.float32)
    return dict(layer_inputs=layer_inputs, out_grads=out_grads, error_prev=error_prev, q_start=q_start)


def unfold_rows(seqs, spacing):
    length = seqs.shape[1]
    padded = jnp.pad(seqs, ((0, 0), (spacing, spacing), (0, 0)))
    pieces = [padded[:, offset * spacing:offset * spacing + length] for offset in range(3)]
    return jnp.concatenate(pieces, axis=2)

def layer_grads(seqs, grads_out, errors, spacing, scale):
    columns = unfold_rows(seqs, spacing).reshape(-1, 3 * C)
    flat_grads = grads_out.reshape(-1, C)
    product = lax.dot_general(columns.astype(jnp.float32), flat_grads.astype(jnp.float32), (((0,), (0,)), ((), ())), preferred_element_type=jnp.float32)
    return product * scale + errors.astype(jnp.float32)

def reference(layer_inputs, out_grads, error_prev, q_start):
    seq_dev = layer_inputs.shape[1] // N_DP
    scale = 1.0 / math.sqrt(seq_dev * LEN)
    rows_three = 3 * C
    high = lax.Precision.HIGHEST
    panel_list = []
    factor_list = []
    error_list = []
    for layer_no in range(LAYERS):
        spacing = DILATION // 2 ** (LAYERS - 1 - layer_no)
        inputs_dev = layer_inputs[layer_no].reshape(N_DP, seq_dev, LEN, C)
        grads_dev = out_grads[layer_no].reshape(N_DP, seq_dev, LEN, C)
        errors_dev = error_prev[layer_no].reshape(N_DP, rows_three, C)

        def one_device(packed):
            return layer_grads(packed[0], packed[1], packed[2], spacing, scale)
        grads_all = lax.map(one_device, (inputs_dev, grads_dev, errors_dev))
        summed = jnp.einsum('jrc,ck->rk', grads_all, q_start[layer_no], precision=high) / math.sqrt(N_DP)
        gram = jnp.dot(summed.T, summed, precision=high) / rows_three
        lower = jnp.linalg.cholesky(gram)
        panel = lax.linalg.triangular_solve(lower, summed, left_side=False, lower=True, transpose_a=True)
        factor = jnp.einsum('jrc,rk->ck', grads_all, panel, precision=high) / math.sqrt(rows_three * N_DP)
        approx = jnp.dot(panel, factor.T, precision=high) / math.sqrt(rows_three * N_DP)
        error_new = (grads_all - approx[None]).astype(jnp.bfloat16).reshape(N_DP * rows_three, C)
        panel_list.append(panel)
        factor_list.append(factor)
        error_list.append(error_new)
    return (jnp.stack(panel_list), jnp.stack(factor_list), jnp.stack(error_list))
```

```python
import functools
import math

import jax
import jax.numpy as jnp
from jax import lax
from jax.experimental import pallas as pl
from jax.experimental.pallas import tpu as pltpu
from jax.sharding import PartitionSpec as P

C = 512
RANK = 64
LEN = 1344
LAYERS = 2
DILATION = 64
PAD = 64
HALF = RANK // 2
F32 = jnp.float32
BF16 = jnp.bfloat16
HIGH = lax.Precision.HIGHEST
VMEM_LIMIT = 56 << 20


def first_bits(devices):
    bits = list(range(1, devices.bit_length() - 1))
    return bits, bits[1:] + bits[:1]


def dot_nn(a, b):
    return lax.dot_general(a, b, (((1,), (0,)), ((), ())), preferred_element_type=F32)


def dot_nt(a, b):
    return lax.dot_general(a, b, (((1,), (1,)), ((), ())), preferred_element_type=F32)


def dot_tn(a, b):
    return lax.dot_general(a, b, (((0,), (0,)), ((), ())), preferred_element_type=F32)


def split2(v):
    hi = v.astype(BF16)
    return hi, (v - hi.astype(F32)).astype(BF16)


def place(devices, which):
    me = lax.axis_index("dp")
    core = lax.rem(me, 2)
    layer = core if which == 0 else 1 - core
    orders = first_bits(devices)
    shift = jnp.where(layer == 0, orders[0][0], orders[1][0])
    return layer, (me >> shift) & 1


def kernel_sums(devices, which, x_hbm, o_hbm, e_hbm, q_ref, out_ref, x_buf, o_buf, e_buf, sems):
    layer, keep = place(devices, which)
    copies = [
        pltpu.make_async_copy(o_hbm.at[layer, 0], o_buf.at[pl.ds(0, LEN)], sems.at[0]),
        pltpu.make_async_copy(x_hbm.at[layer, 0], x_buf.at[pl.ds(0, LEN)], sems.at[1]),
        pltpu.make_async_copy(e_hbm.at[layer], e_buf, sems.at[2]),
    ]
    for copy in copies:
        copy.start()
    o_buf[pl.ds(LEN, PAD)] = jnp.zeros((PAD, C), BF16)
    x_buf[pl.ds(LEN, PAD)] = jnp.zeros((PAD, C), BF16)
    q_t = q_ref[layer].T * (1.0 / math.sqrt(devices))
    q_hi, q_rest = q_t.astype(BF16), None
    q_rest = q_t - q_hi.astype(F32)
    q_mid = q_rest.astype(BF16)
    q_low = (q_rest - q_mid.astype(F32)).astype(BF16)
    q_all = jnp.concatenate([q_hi, q_mid, q_low], axis=0)
    copies[0].wait()
    oq_all = dot_nt(q_all, o_buf[...])
    oq = (oq_all[:RANK] + oq_all[RANK : 2 * RANK] + oq_all[2 * RANK :]) * (1.0 / math.sqrt(LEN))
    spacing = (DILATION // 2) * (1 + layer)
    width = LEN + PAD
    pieces = []
    for shifted in (pltpu.roll(oq, width - spacing, 1), oq, pltpu.roll(oq, spacing, 1)):
        pieces.extend(split2(shifted))
    lhs = jnp.concatenate(pieces, axis=0)
    copies[1].wait()
    prod = dot_nn(lhs, x_buf[...])
    copies[2].wait()
    for k in range(3):
        eq_all = dot_nt(q_all, e_buf[pl.ds(k * C, C)])
        eq = eq_all[:RANK] + eq_all[RANK : 2 * RANK] + eq_all[2 * RANK :]
        total = prod[k * 128 : k * 128 + RANK] + prod[k * 128 + RANK : k * 128 + 128] + eq
        for half in range(2):
            slot = jnp.where(keep == half, 1, 0)
            out_ref[slot, k] = total[half * HALF : (half + 1) * HALF]


def sums(devices, which, x, o, e, q):
    any_spec = pl.BlockSpec(memory_space=pl.ANY)
    vmem = pl.BlockSpec(memory_space=pltpu.VMEM)
    return pl.pallas_call(
        functools.partial(kernel_sums, devices, which),
        out_shape=jax.ShapeDtypeStruct((2, 3, HALF, C), F32),
        in_specs=[any_spec, any_spec, any_spec, vmem],
        out_specs=vmem,
        scratch_shapes=[
            pltpu.VMEM((LEN + PAD, C), BF16),
            pltpu.VMEM((LEN + PAD, C), BF16),
            pltpu.VMEM((3 * C, C), BF16),
            pltpu.SemaphoreType.DMA((3,)),
        ],
        compiler_params=pltpu.CompilerParams(vmem_limit_bytes=VMEM_LIMIT),
        name=f"sums_{which}",
    )(x, o, e, q)


def kernel_grads(devices, which, x_hbm, o_hbm, e_hbm, tie_ref, g_ref, hi_ref, lo_ref, x_buf, o_buf, e_buf, sems):
    layer, _ = place(devices, which)
    copies = [
        pltpu.make_async_copy(x_hbm.at[layer, 0], x_buf, sems.at[0]),
        pltpu.make_async_copy(o_hbm.at[layer, 0], o_buf.at[pl.ds(PAD, LEN)], sems.at[1]),
        pltpu.make_async_copy(e_hbm.at[layer], e_buf, sems.at[2]),
    ]
    for copy in copies:
        copy.start()
    o_buf[pl.ds(0, PAD)] = jnp.zeros((PAD, C), BF16)
    o_buf[pl.ds(PAD + LEN, PAD)] = jnp.zeros((PAD, C), BF16)
    spacing = (DILATION // 2) * (1 + layer)
    for copy in copies:
        copy.wait()
    for k in range(3):
        start = pl.multiple_of(PAD - (k - 1) * spacing, 32)
        prod = dot_tn(x_buf[...], o_buf[pl.ds(start, LEN)])
        rows = pl.ds(k * C, C)
        g = prod * (1.0 / math.sqrt(LEN)) + e_buf[rows].astype(F32)
        g_ref[rows] = g
        hi, lo = split2(g)
        hi_ref[rows] = hi
        lo_ref[rows] = lo


def grads(devices, which, x, o, e, tie):
    any_spec = pl.BlockSpec(memory_space=pl.ANY)
    vmem = pl.BlockSpec(memory_space=pltpu.VMEM)
    return pl.pallas_call(
        functools.partial(kernel_grads, devices, which),
        out_shape=[
            jax.ShapeDtypeStruct((3 * C, C), F32),
            jax.ShapeDtypeStruct((3 * C, C), BF16),
            jax.ShapeDtypeStruct((3 * C, C), BF16),
        ],
        in_specs=[any_spec, any_spec, any_spec, any_spec],
        out_specs=[vmem, vmem, vmem],
        scratch_shapes=[
            pltpu.VMEM((LEN, C), BF16),
            pltpu.VMEM((LEN + 2 * PAD, C), BF16),
            pltpu.VMEM((3 * C, C), BF16),
            pltpu.SemaphoreType.DMA((3,)),
        ],
        compiler_params=pltpu.CompilerParams(vmem_limit_bytes=VMEM_LIMIT),
        name=f"grads_{which}",
    )(x, o, e, tie)


def kernel_right(devices, which, kept_ref, sent_ref, hi_ref, lo_ref, f_ref):
    _, keep = place(devices, which)
    acc = jnp.zeros((2 * RANK, C), F32)
    acc_low = jnp.zeros((RANK, C), F32)
    for k in range(3):
        s = jnp.concatenate([kept_ref[k], sent_ref[k]], axis=0)
        s_hi, s_lo = split2(s)
        rows = pl.ds(k * C, C)
        acc += dot_nn(jnp.concatenate([s_hi, s_lo], axis=0), hi_ref[rows])
        acc_low += dot_nn(s_hi, lo_ref[rows])
    f = acc[:RANK] + acc[RANK:] + acc_low
    f_ref[pl.ds(pl.multiple_of(keep * HALF, HALF), HALF)] = f[:HALF]
    f_ref[pl.ds(pl.multiple_of((1 - keep) * HALF, HALF), HALF)] = f[HALF:]


def right(devices, which, kept, sent, hi, lo):
    vmem = pl.BlockSpec(memory_space=pltpu.VMEM)
    return pl.pallas_call(
        functools.partial(kernel_right, devices, which),
        out_shape=jax.ShapeDtypeStruct((RANK, C), F32),
        in_specs=[vmem] * 4,
        out_specs=vmem,
        compiler_params=pltpu.CompilerParams(vmem_limit_bytes=VMEM_LIMIT),
        name=f"right_{which}",
    )(kept, sent, hi, lo)


def kernel_factor(devices, kept0_ref, sent0_ref, kept1_ref, sent1_ref, inv_ref, p_ref, pp0_ref, pp1_ref, s_buf):
    mats = []
    layers = []
    eye = (
        lax.broadcasted_iota(jnp.int32, (RANK, RANK), 0) == lax.broadcasted_iota(jnp.int32, (RANK, RANK), 1)
    ).astype(F32)
    for which, kept_ref, sent_ref in ((0, kept0_ref, sent0_ref), (1, kept1_ref, sent1_ref)):
        layer, keep = place(devices, which)
        layers.append(layer)
        for k in range(3):
            s_buf[which, k, pl.ds(pl.multiple_of(keep * HALF, HALF), HALF)] = kept_ref[k]
            s_buf[which, k, pl.ds(pl.multiple_of((1 - keep) * HALF, HALF), HALF)] = sent_ref[k]
        gram = jnp.zeros((RANK, RANK), F32)
        for k in range(3):
            s = s_buf[which, k]
            gram += lax.dot_general(s, s, (((1,), (1,)), ((), ())), precision=HIGH, preferred_element_type=F32)
        mats.append(jnp.concatenate([gram * (1.0 / (3 * C)), eye], axis=1))
    row_no = lax.broadcasted_iota(jnp.int32, (RANK, 1), 0)
    for j in range(RANK):
        for which in range(2):
            m = mats[which]
            row = m[j : j + 1, :]
            scaled = row / row[:, j : j + 1]
            col = jnp.where(row_no > j, m[:, j : j + 1], 0.0)
            mats[which] = m - col * scaled
    for which, pp_ref in ((0, pp0_ref), (1, pp1_ref)):
        m = mats[which]
        diag = jnp.sum(m[:, :RANK] * eye, axis=1, keepdims=True)
        inv = m[:, RANK:] * (1.0 / jnp.sqrt(diag))
        inv_ref[which] = inv
        for k in range(3):
            p_t = lax.dot_general(
                inv, s_buf[which, k], (((1,), (0,)), ((), ())), precision=HIGH, preferred_element_type=F32
            )
            p = p_t.T
            p_ref[layers[which], pl.ds(k * C, C)] = p
            hi, lo = split2(p)
            pp_ref[pl.ds(k * C, C)] = jnp.concatenate([hi, lo, hi], axis=1)


def factor(devices, kept0, sent0, kept1, sent1):
    vmem = pl.BlockSpec(memory_space=pltpu.VMEM)
    return pl.pallas_call(
        functools.partial(kernel_factor, devices),
        out_shape=[
            jax.ShapeDtypeStruct((LAYERS, RANK, RANK), F32),
            jax.ShapeDtypeStruct((LAYERS, 3 * C, RANK), F32),
            jax.ShapeDtypeStruct((3 * C, 3 * RANK), BF16),
            jax.ShapeDtypeStruct((3 * C, 3 * RANK), BF16),
        ],
        in_specs=[vmem] * 4,
        out_specs=[vmem] * 4,
        scratch_shapes=[pltpu.VMEM((LAYERS, 3, RANK, C), F32)],
        compiler_params=pltpu.CompilerParams(vmem_limit_bytes=VMEM_LIMIT),
        name="factor",
    )(kept0, sent0, kept1, sent1)


def kernel_errors(devices, f0_ref, f1_ref, inv_ref, pp0_ref, pp1_ref, g0_ref, g1_ref, factor_ref, err_hbm, err_buf, sems):
    norm = 1.0 / math.sqrt(3 * C * devices)
    copies = []
    for which, f_ref, pp_ref, g_ref in ((0, f0_ref, pp0_ref, g0_ref), (1, f1_ref, pp1_ref, g1_ref)):
        layer, _ = place(devices, which)
        f_t = (
            lax.dot_general(
                inv_ref[which], f_ref[...], (((1,), (0,)), ((), ())), precision=HIGH, preferred_element_type=F32
            )
            * norm
        )
        factor_ref[layer] = f_t.T
        hi, lo = split2(f_t * norm)
        rhs = jnp.concatenate([hi, hi, lo], axis=0)
        for k in range(3):
            rows = pl.ds(k * C, C)
            err_buf[which, rows] = (g_ref[rows] - dot_nn(pp_ref[rows], rhs)).astype(BF16)
            copy = pltpu.make_async_copy(err_buf.at[which, rows], err_hbm.at[layer, rows], sems.at[which, k])
            copy.start()
            copies.append(copy)
    for copy in copies:
        copy.wait()


def errors(devices, f0, f1, inv, pp0, pp1, g0, g1):
    vmem = pl.BlockSpec(memory_space=pltpu.VMEM)
    return pl.pallas_call(
        functools.partial(kernel_errors, devices),
        out_shape=[
            jax.ShapeDtypeStruct((LAYERS, C, RANK), F32),
            jax.ShapeDtypeStruct((LAYERS, 3 * C, C), BF16),
        ],
        in_specs=[vmem] * 7,
        out_specs=[vmem, pl.BlockSpec(memory_space=pl.ANY)],
        scratch_shapes=[pltpu.VMEM((LAYERS, 3 * C, C), BF16), pltpu.SemaphoreType.DMA((2, 3))],
        compiler_params=pltpu.CompilerParams(vmem_limit_bytes=VMEM_LIMIT),
        name="errors",
    )(f0, f1, inv, pp0, pp1, g0, g1)


def body(devices, x, o, e, q):
    orders = first_bits(devices)
    steps = len(orders[0])

    def swap_core(v):
        return lax.ppermute(v, "dp", [(i, i ^ 1) for i in range(devices)])

    def swap(v, step):
        return lax.ppermute(v, "dp", [(i, i ^ (1 << orders[i & 1][step])) for i in range(devices)])

    other = sums(devices, 1, x, o, e, q)
    got = swap_core(other)
    own = sums(devices, 0, x, o, e, q)
    chip = own + got
    part = chip[1] + swap(chip[0], 0)
    g0, hi0, lo0 = grads(devices, 0, x, o, e, own)
    g1, hi1, lo1 = grads(devices, 1, x, o, e, part)
    for step in range(1, steps):
        part = part + swap(part, step)
    kept0 = part
    sent0 = swap(part, 0)
    kept1 = swap_core(kept0)
    sent1 = swap_core(sent0)
    f0 = right(devices, 0, kept0, sent0, hi0, lo0)
    f1 = right(devices, 1, kept1, sent1, hi1, lo1)
    f0 = f0 + swap_core(f1)
    inv, panel, pp0, pp1 = factor(devices, kept0, sent0, kept1, sent1)
    for step in range(steps):
        f0 = f0 + swap(f0, step)
    f1 = swap_core(f0)
    factors, error = errors(devices, f0, f1, inv, pp0, pp1, g0, g1)
    return panel, factors, error


def solution(mesh):
    devices = mesh.shape["dp"]
    in_specs = (
        P(None, ("groups", "dp"), None, None),
        P(None, ("groups", "dp"), None, None),
        P(None, ("groups", "dp"), None),
        P(),
    )
    out_specs = (P("groups", None, None), P("groups", None, None), P(None, ("groups", "dp"), None))
    return jax.shard_map(
        functools.partial(body, devices), mesh=mesh, in_specs=in_specs, out_specs=out_specs, check_vma=False
    )
```

```python
import functools
import math

import jax
import jax.numpy as jnp
from jax import lax
from jax.experimental import pallas as pl
from jax.experimental.pallas import tpu as pltpu
from jax.sharding import PartitionSpec as P

C = 512
RANK = 64
LEN = 1344
LAYERS = 2
DILATION = 64
PAD = 64
STREAMS = 2
PART = RANK // (2 * STREAMS)
F32 = jnp.float32
BF16 = jnp.bfloat16
HIGH = lax.Precision.HIGHEST
VMEM_LIMIT = 14 << 20
CUTS = (18, 44)
PLAN = [((0, 0), (0, 1)), ((0, 2), (1, 0)), ((1, 1), (1, 2))]


def exchange_bits(devices):
    bits = list(range(1, devices.bit_length() - 1))
    return bits, bits[1:] + bits[:1]


def dot_nn(a, b):
    return lax.dot_general(a, b, (((1,), (0,)), ((), ())), preferred_element_type=F32)


def dot_nt(a, b):
    return lax.dot_general(a, b, (((1,), (1,)), ((), ())), preferred_element_type=F32)


def dot_tn(a, b):
    return lax.dot_general(a, b, (((0,), (0,)), ((), ())), preferred_element_type=F32)


def split2(v):
    hi = v.astype(BF16)
    return hi, (v - hi.astype(F32)).astype(BF16)


def place(which):
    core = lax.rem(lax.axis_index("dp"), 2)
    return core if which == 0 else 1 - core


def kept(devices, layer):
    orders = exchange_bits(devices)
    return (lax.axis_index("dp") >> jnp.where(layer == 0, orders[0][0], orders[1][0])) & 1


def spec(space):
    return pl.BlockSpec(memory_space=space)


def local(v):
    return pltpu.with_memory_space_constraint(v, pltpu.VMEM)


def far(v):
    return pltpu.with_memory_space_constraint(v, pltpu.HBM)


def cost(flops, nbytes):
    return pl.CostEstimate(flops=flops, transcendentals=0, bytes_accessed=nbytes)


def layer_sum(devices, layer, q_ref, x_ref, o_ref, e_ref, waits, out_ref):
    keep = kept(devices, layer)
    q_t = q_ref[layer] * (1.0 / math.sqrt(devices))
    q_hi = q_t.astype(BF16)
    q_mid, q_low = split2(q_t - q_hi.astype(F32))
    q_all = jnp.concatenate([q_hi, q_mid, q_low], axis=0)
    waits[0]()
    oq_all = dot_nt(q_all, o_ref[pl.ds(PAD, LEN + PAD)])
    oq = (oq_all[:RANK] + oq_all[RANK : 2 * RANK] + oq_all[2 * RANK :]) * (1.0 / math.sqrt(LEN))
    spacing = (DILATION // 2) * (1 + layer)
    width = LEN + PAD
    pieces = []
    for shifted in (pltpu.roll(oq, width - spacing, 1), oq, pltpu.roll(oq, spacing, 1)):
        pieces.extend(split2(shifted))
    lhs = jnp.concatenate(pieces, axis=0)
    waits[1]()
    prod = dot_nn(lhs, x_ref[...])
    waits[2]()
    for k in range(3):
        eq_all = dot_nt(q_all, e_ref[pl.ds(k * C, C)])
        eq = eq_all[:RANK] + eq_all[RANK : 2 * RANK] + eq_all[2 * RANK :]
        total = prod[k * 128 : k * 128 + RANK] + prod[k * 128 + RANK : k * 128 + 128] + eq
        for i in range(2 * STREAMS):
            slot = jnp.where(keep == i % 2, 1, 0)
            out_ref[slot, i // 2, k] = total[i * PART : (i + 1) * PART]


def kernel_load(devices, x_hbm, o_hbm, e_hbm, q_hbm, out_ref, x1, o1, e1, x0, o0, e0, q_ref, sems):
    copies = [pltpu.make_async_copy(q_hbm, q_ref, sems.at[2, 0])]
    for which, x_ref, o_ref, e_ref in ((1, x1, o1, e1), (0, x0, o0, e0)):
        layer = place(which)
        copies += [
            pltpu.make_async_copy(o_hbm.at[layer, 0], o_ref.at[pl.ds(PAD, LEN)], sems.at[which, 0]),
            pltpu.make_async_copy(x_hbm.at[layer, 0], x_ref.at[pl.ds(0, LEN)], sems.at[which, 1]),
            pltpu.make_async_copy(e_hbm.at[layer], e_ref, sems.at[which, 2]),
        ]
    for copy in copies:
        copy.start()
    zeros = jnp.zeros((PAD, C), BF16)
    for x_ref, o_ref in ((x1, o1), (x0, o0)):
        o_ref[pl.ds(0, PAD)] = zeros
        o_ref[pl.ds(PAD + LEN, PAD)] = zeros
        x_ref[pl.ds(LEN, PAD)] = zeros
    copies[0].wait()
    layer_sum(devices, place(1), q_ref, x1, o1, e1, [copy.wait for copy in copies[1:4]], out_ref)
    for copy in copies[4:]:
        copy.wait()


def load(devices, x, o, e, q):
    return pl.pallas_call(
        functools.partial(kernel_load, devices),
        out_shape=[
            pltpu.VMEM((2, STREAMS, 3, PART, C), F32),
            pltpu.VMEM((LEN + PAD, C), BF16),
            pltpu.VMEM((LEN + 2 * PAD, C), BF16),
            pltpu.VMEM((3 * C, C), BF16),
            pltpu.VMEM((LEN + PAD, C), BF16),
            pltpu.VMEM((LEN + 2 * PAD, C), BF16),
            pltpu.VMEM((3 * C, C), BF16),
            pltpu.VMEM((LAYERS, RANK, C), F32),
        ],
        in_specs=[spec(pltpu.HBM)] * 4,
        out_specs=[spec(pltpu.VMEM)] * 8,
        scratch_shapes=[pltpu.SemaphoreType.DMA((3, 3))],
        compiler_params=pltpu.CompilerParams(vmem_limit_bytes=VMEM_LIMIT),
        cost_estimate=cost(2 * 10**9, 9 * 10**6),
        name="load",
    )(far(x), far(o), far(e), far(q))


def kernel_sums(devices, q_ref, x_ref, o_ref, e_ref, out_ref):
    layer_sum(devices, place(0), q_ref, x_ref, o_ref, e_ref, [lambda: None] * 3, out_ref)


def sums(devices, q, x, o, e):
    return pl.pallas_call(
        functools.partial(kernel_sums, devices),
        out_shape=pltpu.VMEM((2, STREAMS, 3, PART, C), F32),
        in_specs=[spec(pltpu.VMEM)] * 4,
        out_specs=spec(pltpu.VMEM),
        compiler_params=pltpu.CompilerParams(vmem_limit_bytes=VMEM_LIMIT),
        cost_estimate=cost(2 * 10**9, 4 * 10**6),
        name="sums",
    )(local(q), local(x), local(o), local(e))


def kernel_grads(parts, *refs):
    ins, outs = refs[: 3 * len(parts)], refs[3 * len(parts) + 1 :]
    for i, (which, k) in enumerate(parts):
        x_ref, o_ref, e_ref = ins[3 * i : 3 * i + 3]
        g_ref, hi_ref, lo_ref = outs[3 * i : 3 * i + 3]
        spacing = (DILATION // 2) * (1 + place(which))
        start = pl.multiple_of(PAD - (k - 1) * spacing, 32)
        prod = dot_tn(x_ref[pl.ds(0, LEN)], o_ref[pl.ds(start, LEN)])
        g = prod * (1.0 / math.sqrt(LEN)) + e_ref[pl.ds(k * C, C)].astype(F32)
        g_ref[...] = g
        hi_ref[...], lo_ref[...] = split2(g)
    outs[-1][...] = jnp.zeros_like(outs[-1])


def grads(parts, arrays, tie):
    ins = [local(v) for which, _ in parts for v in arrays[which]]
    block = [pltpu.VMEM((C, C), F32), pltpu.VMEM((C, C), BF16), pltpu.VMEM((C, C), BF16)]
    out = pl.pallas_call(
        functools.partial(kernel_grads, parts),
        out_shape=block * len(parts) + [pltpu.VMEM((3, PART, C), F32)],
        in_specs=[spec(pltpu.VMEM)] * len(ins) + [spec(pl.ANY)],
        out_specs=[spec(pltpu.VMEM)] * (3 * len(parts) + 1),
        compiler_params=pltpu.CompilerParams(vmem_limit_bytes=VMEM_LIMIT),
        cost_estimate=cost(10**9 * len(parts), 3 * 10**6 * len(parts)),
        name="grads_" + "_".join(f"{which}{k}" for which, k in parts),
    )(*ins, tie)
    return {part: out[3 * i : 3 * i + 3] for i, part in enumerate(parts)}, out[-1]


def gather_parts(devices, which, part_refs, k):
    keep = kept(devices, place(which))
    rows = [(2 * (i // 2) + (keep if i % 2 == 0 else 1 - keep)) * PART for i in range(2 * STREAMS)]
    return [ref[k] for ref in part_refs], [pl.multiple_of(row, PART) for row in rows]


def kernel_right(devices, which, *refs):
    part_refs, his, los, f_ref = refs[: 2 * STREAMS], refs[2 * STREAMS :][:3], refs[2 * STREAMS + 3 :][:3], refs[-1]
    acc = jnp.zeros((2 * RANK, C), F32)
    acc_low = jnp.zeros((RANK, C), F32)
    for k in range(3):
        parts, rows = gather_parts(devices, which, part_refs, k)
        s_hi, s_lo = split2(jnp.concatenate(parts, axis=0))
        acc += dot_nn(jnp.concatenate([s_hi, s_lo], axis=0), his[k][...])
        acc_low += dot_nn(s_hi, los[k][...])
    f = acc[:RANK] + acc[RANK:] + acc_low
    for i, row in enumerate(rows):
        f_ref[pl.ds(row, PART)] = f[i * PART : (i + 1) * PART]


def right(devices, which, parts, blocks):
    his = [local(blocks[which, k][1]) for k in range(3)]
    los = [local(blocks[which, k][2]) for k in range(3)]
    return pl.pallas_call(
        functools.partial(kernel_right, devices, which),
        out_shape=pltpu.VMEM((RANK, C), F32),
        in_specs=[spec(pltpu.VMEM)] * (2 * STREAMS + 6),
        out_specs=spec(pltpu.VMEM),
        compiler_params=pltpu.CompilerParams(vmem_limit_bytes=VMEM_LIMIT),
        cost_estimate=cost(10**9, 4 * 10**6),
        name=f"right_{which}",
    )(*parts, *his, *los)


def eliminate(mats, first, last):
    row_no = lax.broadcasted_iota(jnp.int32, (RANK, 1), 0)
    mats = list(mats)
    for j in range(first, last):
        for which in range(2):
            m = mats[which]
            row = m[j : j + 1, :]
            scaled = row / row[:, j : j + 1]
            col = jnp.where(row_no > j, m[:, j : j + 1], 0.0)
            mats[which] = m - col * scaled
    return mats


def kernel_gram(devices, last, *refs):
    s_ref, m_ref, token_ref = refs[-3:]
    mats = []
    eye = (
        lax.broadcasted_iota(jnp.int32, (RANK, RANK), 0) == lax.broadcasted_iota(jnp.int32, (RANK, RANK), 1)
    ).astype(F32)
    for which in range(2):
        for k in range(3):
            parts, rows = gather_parts(devices, which, refs[which * 2 * STREAMS :][: 2 * STREAMS], k)
            for part, row in zip(parts, rows):
                s_ref[which, k, pl.ds(row, PART)] = part
        gram = jnp.zeros((RANK, RANK), F32)
        for k in range(3):
            s = s_ref[which, k]
            gram += lax.dot_general(s, s, (((1,), (1,)), ((), ())), precision=HIGH, preferred_element_type=F32)
        mats.append(jnp.concatenate([gram * (1.0 / (3 * C)), eye], axis=1))
    mats = eliminate(mats, 0, last)
    for which in range(2):
        m_ref[which] = mats[which]
    token_ref[...] = jnp.zeros_like(token_ref)


def gram(devices, last, parts, tie):
    return pl.pallas_call(
        functools.partial(kernel_gram, devices, last),
        out_shape=[
            pltpu.VMEM((LAYERS, 3, RANK, C), F32),
            pltpu.VMEM((LAYERS, RANK, 2 * RANK), F32),
            pltpu.VMEM((RANK, C), F32),
        ],
        in_specs=[spec(pltpu.VMEM)] * len(parts) + [spec(pl.ANY)],
        out_specs=[spec(pltpu.VMEM)] * 3,
        compiler_params=pltpu.CompilerParams(vmem_limit_bytes=VMEM_LIMIT),
        cost_estimate=cost(2 * 10**9, 10 * 10**6),
        name="gram",
    )(*parts, tie)


def kernel_middle(first, last, m_ref, tie_ref, out_ref, token_ref):
    mats = eliminate([m_ref[0], m_ref[1]], first, last)
    for which in range(2):
        out_ref[which] = mats[which]
    token_ref[...] = jnp.zeros_like(token_ref)


def middle(first, last, m, tie):
    return pl.pallas_call(
        functools.partial(kernel_middle, first, last),
        out_shape=[pltpu.VMEM((LAYERS, RANK, 2 * RANK), F32), pltpu.VMEM((RANK, C), F32)],
        in_specs=[spec(pltpu.VMEM), spec(pl.ANY)],
        out_specs=[spec(pltpu.VMEM)] * 2,
        compiler_params=pltpu.CompilerParams(vmem_limit_bytes=VMEM_LIMIT),
        cost_estimate=cost(2 * 10**9, 10 * 10**6),
        name=f"middle_{first}",
    )(local(m), tie)


def kernel_panels(first, s_ref, m_ref, tie_ref, inv_ref, p_ref, pp_ref, token_ref):
    mats = eliminate([m_ref[0], m_ref[1]], first, RANK)
    eye = (
        lax.broadcasted_iota(jnp.int32, (RANK, RANK), 0) == lax.broadcasted_iota(jnp.int32, (RANK, RANK), 1)
    ).astype(F32)
    for which in range(2):
        layer = place(which)
        m = mats[which]
        diag = jnp.sum(m[:, :RANK] * eye, axis=1, keepdims=True)
        inv = m[:, RANK:] * (1.0 / jnp.sqrt(diag))
        inv_ref[which] = inv
        for k in range(3):
            p_t = lax.dot_general(
                inv, s_ref[which, k], (((1,), (0,)), ((), ())), precision=HIGH, preferred_element_type=F32
            )
            p_ref[layer, :, pl.ds(k * C, C)] = p_t
            hi, lo = split2(p_t.T)
            pp_ref[which, pl.ds(k * C, C)] = jnp.concatenate([hi, lo, hi], axis=1)
    token_ref[...] = jnp.zeros_like(token_ref)


def panels(first, s, m, tie):
    return pl.pallas_call(
        functools.partial(kernel_panels, first),
        out_shape=[
            pltpu.VMEM((LAYERS, RANK, RANK), F32),
            jax.ShapeDtypeStruct((LAYERS, RANK, 3 * C), F32),
            pltpu.VMEM((LAYERS, 3 * C, 3 * RANK), BF16),
            pltpu.VMEM((RANK, C), F32),
        ],
        in_specs=[spec(pltpu.VMEM), spec(pltpu.VMEM), spec(pl.ANY)],
        out_specs=[spec(pltpu.VMEM)] * 4,
        compiler_params=pltpu.CompilerParams(vmem_limit_bytes=VMEM_LIMIT),
        cost_estimate=cost(2 * 10**9, 10 * 10**6),
        name="panels",
    )(local(s), local(m), tie)


def layer_error(devices, which, f_ref, inv_ref, pp_ref, g_refs, err_ref, each):
    norm = 1.0 / math.sqrt(3 * C * devices)
    f_t = (
        lax.dot_general(
            inv_ref[which], f_ref[...], (((1,), (0,)), ((), ())), precision=HIGH, preferred_element_type=F32
        )
        * norm
    )
    hi, lo = split2(f_t * norm)
    rhs = jnp.concatenate([hi, hi, lo], axis=0)
    for k in range(3):
        rows = pl.ds(k * C, C)
        err_ref[rows] = (g_refs[k][...] - dot_nn(pp_ref[which, rows], rhs)).astype(BF16)
        each(k)
    return f_t


def kernel_own_error(devices, f_ref, inv_ref, pp_ref, g0, g1, g2, factor_ref, err_ref):
    factor_ref[...] = layer_error(devices, 0, f_ref, inv_ref, pp_ref, (g0, g1, g2), err_ref, lambda k: None)


def kernel_errors(devices, f_ref, inv_ref, pp_ref, g0, g1, g2, own_factor, own_err, factor_ref, err_hbm, err_ref, sems):
    copies = []

    def write(source, which, k):
        rows = pl.ds(k * C, C)
        copy = pltpu.make_async_copy(source.at[rows], err_hbm.at[place(which), rows], sems.at[which, k])
        copy.start()
        copies.append(copy)

    for k in range(3):
        write(own_err, 0, k)
    factor_ref[place(0)] = own_factor[...]
    factor_ref[place(1)] = layer_error(
        devices, 1, f_ref, inv_ref, pp_ref, (g0, g1, g2), err_ref, lambda k: write(err_ref, 1, k)
    )
    for copy in copies:
        copy.wait()


def own_error(devices, f, inv, pp, blocks):
    return pl.pallas_call(
        functools.partial(kernel_own_error, devices),
        out_shape=[pltpu.VMEM((RANK, C), F32), pltpu.VMEM((3 * C, C), BF16)],
        in_specs=[spec(pltpu.VMEM)] * 6,
        out_specs=[spec(pltpu.VMEM)] * 2,
        compiler_params=pltpu.CompilerParams(vmem_limit_bytes=VMEM_LIMIT),
        cost_estimate=cost(10**9, 5 * 10**6),
        name="own_error",
    )(f, local(inv), local(pp), *[local(blocks[0, k][0]) for k in range(3)])


def errors(devices, f, inv, pp, blocks, own_factor, own_err):
    return pl.pallas_call(
        functools.partial(kernel_errors, devices),
        out_shape=[jax.ShapeDtypeStruct((LAYERS, RANK, C), F32), pltpu.HBM((LAYERS, 3 * C, C), BF16)],
        in_specs=[spec(pltpu.VMEM)] * 8,
        out_specs=[spec(pltpu.VMEM), spec(pltpu.HBM)],
        scratch_shapes=[pltpu.VMEM((3 * C, C), BF16), pltpu.SemaphoreType.DMA((2, 3))],
        compiler_params=pltpu.CompilerParams(vmem_limit_bytes=VMEM_LIMIT),
        cost_estimate=cost(10**9, 5 * 10**6),
        name="errors",
    )(f, local(inv), local(pp), *[local(blocks[1, k][0]) for k in range(3)], local(own_factor), local(own_err))


def body(devices, x, o, e, q):
    orders = exchange_bits(devices)
    steps = len(orders[0])

    def swap_core(v):
        return lax.ppermute(v, "dp", [(i, i ^ 1) for i in range(devices)])

    def swap(v, step):
        return lax.ppermute(v, "dp", [(i, i ^ (1 << orders[i & 1][step])) for i in range(devices)])

    q = jnp.swapaxes(q, 1, 2)
    other, x1, o1, e1, x0, o0, e0, q_all = load(devices, x, o, e, q)
    got = swap_core(other)
    own = sums(devices, q_all, x0, o0, e0)
    sent = [own[0, i] + got[0, i] for i in range(STREAMS)]
    held = [own[1, i] + got[1, i] for i in range(STREAMS)]
    arrays = ((x0, o0, e0), (x1, o1, e1))
    blocks = {}
    plan = PLAN if steps + 1 >= len(PLAN) else [sum(PLAN, ())]
    for step in range(steps + 1):
        if step == 0:
            arrived = [swap(v, 0) for v in sent]
        else:
            arrived = [swap(v, step % steps) for v in held]
        if step < len(plan) and plan[step]:
            formed, token = grads(plan[step], arrays, held[-1])
            blocks.update(formed)
            arrived = [v + token for v in arrived]
        if step < steps:
            held = [v + w for v, w in zip(held, arrived)]
    own_parts = [v for pair in zip(held, arrived) for v in pair]
    other_parts = [swap_core(v) for v in own_parts]
    f0 = right(devices, 0, own_parts, blocks)
    f1 = right(devices, 1, other_parts, blocks)
    f0 = f0 + swap_core(f1)
    s_all, mat, token = gram(devices, CUTS[0], own_parts + other_parts, f0)
    for step in range(steps):
        got = swap(f0, step)
        if step == 1:
            mat, token = middle(CUTS[0], CUTS[1], mat, f0)
        if step == 2:
            inv, panel, pp, token = panels(CUTS[1], s_all, mat, f0)
        if step < 3:
            got = got + token
        f0 = f0 + got
    f1 = swap_core(f0)
    own_factor, own_err = own_error(devices, f0, inv, pp, blocks)
    factors, error = errors(devices, f1, inv, pp, blocks, own_factor, own_err)
    return jnp.swapaxes(panel, 1, 2), jnp.swapaxes(factors, 1, 2), error


def solution(mesh):
    devices = mesh.shape["dp"]
    in_specs = (
        P(None, ("groups", "dp"), None, None),
        P(None, ("groups", "dp"), None, None),
        P(None, ("groups", "dp"), None),
        P(),
    )
    out_specs = (P("groups", None, None), P("groups", None, None), P(None, ("groups", "dp"), None))
    return jax.shard_map(
        functools.partial(body, devices), mesh=mesh, in_specs=in_specs, out_specs=out_specs, check_vma=False
    )
```

```python
import functools
import math

import jax
import jax.numpy as jnp
from jax import lax
from jax.experimental import pallas as pl
from jax.experimental.pallas import tpu as pltpu
from jax.sharding import PartitionSpec as P

C = 512
RANK = 64
LEN = 1344
LAYERS = 2
DILATION = 64
PAD = 64
STREAMS = 2
PART = RANK // (2 * STREAMS)
F32 = jnp.float32
BF16 = jnp.bfloat16
HIGH = lax.Precision.HIGHEST
VMEM_LIMIT = 14 << 20
CUTS = (3, 8)
PLAN = [((0, 0), (0, 1)), ((0, 2), (1, 0)), ((1, 1), (1, 2))]


def exchange_bits(devices):
    bits = list(range(1, devices.bit_length() - 1))
    return bits, bits[1:] + bits[:1]


def dot_nn(a, b):
    return lax.dot_general(a, b, (((1,), (0,)), ((), ())), preferred_element_type=F32)


def dot_nt(a, b):
    return lax.dot_general(a, b, (((1,), (1,)), ((), ())), preferred_element_type=F32)


def dot_tn(a, b):
    return lax.dot_general(a, b, (((0,), (0,)), ((), ())), preferred_element_type=F32)


def split2(v):
    hi = v.astype(BF16)
    return hi, (v - hi.astype(F32)).astype(BF16)


def place(which):
    core = lax.rem(lax.axis_index("dp"), 2)
    return core if which == 0 else 1 - core


def kept(devices, layer):
    orders = exchange_bits(devices)
    return (lax.axis_index("dp") >> jnp.where(layer == 0, orders[0][0], orders[1][0])) & 1


def spec(space):
    return pl.BlockSpec(memory_space=space)


def local(v):
    return pltpu.with_memory_space_constraint(v, pltpu.VMEM)


def far(v):
    return pltpu.with_memory_space_constraint(v, pltpu.HBM)


TOKENS = [pltpu.VMEM((2 * PART, C), F32)] * STREAMS


def clear(refs):
    for ref in refs:
        ref[...] = jnp.zeros_like(ref)


def cost(flops, nbytes):
    return pl.CostEstimate(flops=flops, transcendentals=0, bytes_accessed=nbytes)


def layer_sum(devices, layer, q_ref, x_ref, o_ref, e_ref, waits, out_ref):
    keep = kept(devices, layer)
    q_t = q_ref[layer] * (1.0 / math.sqrt(devices))
    q_hi = q_t.astype(BF16)
    q_mid, q_low = split2(q_t - q_hi.astype(F32))
    q_all = jnp.concatenate([q_hi, q_mid, q_low], axis=0)
    waits[0]()
    oq_all = dot_nt(q_all, o_ref[pl.ds(PAD, LEN + PAD)])
    oq = (oq_all[:RANK] + oq_all[RANK : 2 * RANK] + oq_all[2 * RANK :]) * (1.0 / math.sqrt(LEN))
    spacing = (DILATION // 2) * (1 + layer)
    width = LEN + PAD
    pieces = []
    for shifted in (pltpu.roll(oq, width - spacing, 1), oq, pltpu.roll(oq, spacing, 1)):
        pieces.extend(split2(shifted))
    lhs = jnp.concatenate(pieces, axis=0)
    waits[1]()
    prod = dot_nn(lhs, x_ref[...])
    waits[2]()
    for k in range(3):
        eq_all = dot_nt(q_all, e_ref[pl.ds(k * C, C)])
        eq = eq_all[:RANK] + eq_all[RANK : 2 * RANK] + eq_all[2 * RANK :]
        total = prod[k * 128 : k * 128 + RANK] + prod[k * 128 + RANK : k * 128 + 128] + eq
        for i in range(2 * STREAMS):
            slot = jnp.where(keep == i % 2, 1, 0)
            out_ref[slot, i // 2, k] = total[i * PART : (i + 1) * PART]


def kernel_load(devices, x_hbm, o_hbm, e_hbm, q_hbm, out_ref, x1, o1, e1, x0, o0, e0, q_ref, sems):
    copies = [pltpu.make_async_copy(q_hbm, q_ref, sems.at[2, 0])]
    for which, x_ref, o_ref, e_ref in ((1, x1, o1, e1), (0, x0, o0, e0)):
        layer = place(which)
        copies += [
            pltpu.make_async_copy(o_hbm.at[layer, 0], o_ref.at[pl.ds(PAD, LEN)], sems.at[which, 0]),
            pltpu.make_async_copy(x_hbm.at[layer, 0], x_ref.at[pl.ds(0, LEN)], sems.at[which, 1]),
            pltpu.make_async_copy(e_hbm.at[layer], e_ref, sems.at[which, 2]),
        ]
    for copy in copies:
        copy.start()
    zeros = jnp.zeros((PAD, C), BF16)
    for x_ref, o_ref in ((x1, o1), (x0, o0)):
        o_ref[pl.ds(0, PAD)] = zeros
        o_ref[pl.ds(PAD + LEN, PAD)] = zeros
        x_ref[pl.ds(LEN, PAD)] = zeros
    copies[0].wait()
    layer_sum(devices, place(1), q_ref, x1, o1, e1, [copy.wait for copy in copies[1:4]], out_ref)
    for copy in copies[4:]:
        copy.wait()


def load(devices, x, o, e, q):
    return pl.pallas_call(
        functools.partial(kernel_load, devices),
        out_shape=[
            pltpu.VMEM((2, STREAMS, 3, PART, C), F32),
            pltpu.VMEM((LEN + PAD, C), BF16),
            pltpu.VMEM((LEN + 2 * PAD, C), BF16),
            pltpu.VMEM((3 * C, C), BF16),
            pltpu.VMEM((LEN + PAD, C), BF16),
            pltpu.VMEM((LEN + 2 * PAD, C), BF16),
            pltpu.VMEM((3 * C, C), BF16),
            pltpu.VMEM((LAYERS, RANK, C), F32),
        ],
        in_specs=[spec(pltpu.HBM)] * 4,
        out_specs=[spec(pltpu.VMEM)] * 8,
        scratch_shapes=[pltpu.SemaphoreType.DMA((3, 3))],
        compiler_params=pltpu.CompilerParams(vmem_limit_bytes=VMEM_LIMIT),
        cost_estimate=cost(2 * 10**9, 9 * 10**6),
        name="load",
    )(far(x), far(o), far(e), far(q))


def kernel_sums(devices, q_ref, x_ref, o_ref, e_ref, out_ref):
    layer_sum(devices, place(0), q_ref, x_ref, o_ref, e_ref, [lambda: None] * 3, out_ref)


def sums(devices, q, x, o, e):
    return pl.pallas_call(
        functools.partial(kernel_sums, devices),
        out_shape=pltpu.VMEM((2, STREAMS, 3, PART, C), F32),
        in_specs=[spec(pltpu.VMEM)] * 4,
        out_specs=spec(pltpu.VMEM),
        compiler_params=pltpu.CompilerParams(vmem_limit_bytes=VMEM_LIMIT),
        cost_estimate=cost(2 * 10**9, 4 * 10**6),
        name="sums",
    )(local(q), local(x), local(o), local(e))


def kernel_grads(parts, *refs):
    ins, outs = refs[: 3 * len(parts)], refs[3 * len(parts) + 1 :]
    for i, (which, k) in enumerate(parts):
        x_ref, o_ref, e_ref = ins[3 * i : 3 * i + 3]
        g_ref, hi_ref, lo_ref = outs[3 * i : 3 * i + 3]
        spacing = (DILATION // 2) * (1 + place(which))
        start = pl.multiple_of(PAD - (k - 1) * spacing, 32)
        prod = dot_tn(x_ref[pl.ds(0, LEN)], o_ref[pl.ds(start, LEN)])
        g = prod * (1.0 / math.sqrt(LEN)) + e_ref[pl.ds(k * C, C)].astype(F32)
        g_ref[...] = g
        hi_ref[...], lo_ref[...] = split2(g)
    clear(outs[-STREAMS:])


def grads(parts, arrays, tie):
    ins = [local(v) for which, _ in parts for v in arrays[which]]
    block = [pltpu.VMEM((C, C), F32), pltpu.VMEM((C, C), BF16), pltpu.VMEM((C, C), BF16)]
    out = pl.pallas_call(
        functools.partial(kernel_grads, parts),
        out_shape=block * len(parts) + [pltpu.VMEM((3, PART, C), F32)] * STREAMS,
        in_specs=[spec(pltpu.VMEM)] * len(ins) + [spec(pl.ANY)],
        out_specs=[spec(pltpu.VMEM)] * (3 * len(parts) + STREAMS),
        compiler_params=pltpu.CompilerParams(vmem_limit_bytes=VMEM_LIMIT),
        cost_estimate=cost(10**9 * len(parts), 3 * 10**6 * len(parts)),
        name="grads_" + "_".join(f"{which}{k}" for which, k in parts),
    )(*ins, tie)
    return {part: out[3 * i : 3 * i + 3] for i, part in enumerate(parts)}, out[-STREAMS:]


def kernel_gate(*refs):
    pass


def gate(values, tie):
    n = len(values)
    return pl.pallas_call(
        kernel_gate,
        out_shape=[pltpu.VMEM(v.shape, v.dtype) for v in values],
        in_specs=[spec(pltpu.VMEM)] * n + [spec(pl.ANY)],
        out_specs=[spec(pltpu.VMEM)] * n,
        input_output_aliases={i: i for i in range(n)},
        compiler_params=pltpu.CompilerParams(vmem_limit_bytes=VMEM_LIMIT),
        cost_estimate=cost(0, 0),
        name="gate",
    )(*[local(v) for v in values], tie)


def gather_parts(devices, which, part_refs, k):
    keep = kept(devices, place(which))
    rows = [(2 * (i // 2) + (keep if i % 2 == 0 else 1 - keep)) * PART for i in range(len(part_refs))]
    return [ref[k] for ref in part_refs], [pl.multiple_of(row, PART) for row in rows]


def kernel_right(devices, which, *refs):
    part_refs, his, los, f_refs = refs[: 2 * STREAMS], refs[2 * STREAMS :][:3], refs[2 * STREAMS + 3 :][:3], refs[-STREAMS:]
    acc = jnp.zeros((2 * RANK, C), F32)
    acc_low = jnp.zeros((RANK, C), F32)
    for k in range(3):
        parts, rows = gather_parts(devices, which, part_refs, k)
        s_hi, s_lo = split2(jnp.concatenate(parts, axis=0))
        acc += dot_nn(jnp.concatenate([s_hi, s_lo], axis=0), his[k][...])
        acc_low += dot_nn(s_hi, los[k][...])
    f = acc[:RANK] + acc[RANK:] + acc_low
    for i, row in enumerate(rows):
        row = pl.multiple_of(row - (i // 2) * 2 * PART, PART)
        f_refs[i // 2][pl.ds(row, PART)] = f[i * PART : (i + 1) * PART]


def right(devices, which, parts, blocks):
    his = [local(blocks[which, k][1]) for k in range(3)]
    los = [local(blocks[which, k][2]) for k in range(3)]
    return pl.pallas_call(
        functools.partial(kernel_right, devices, which),
        out_shape=[pltpu.VMEM((2 * PART, C), F32)] * STREAMS,
        in_specs=[spec(pltpu.VMEM)] * (2 * STREAMS + 6),
        out_specs=[spec(pltpu.VMEM)] * STREAMS,
        compiler_params=pltpu.CompilerParams(vmem_limit_bytes=VMEM_LIMIT),
        cost_estimate=cost(10**9, 4 * 10**6),
        name=f"right_{which}",
    )(*parts, *his, *los)


def lanes(v, column):
    return jnp.broadcast_to(v[:, column : column + 1], (8, 128))


def subs(v, row):
    return jnp.broadcast_to(v[row : row + 1, :], (8, 128))


def eliminate(mats, first, last):
    tiles = [[m[8 * i : 8 * i + 8] for i in range(RANK // 8)] for m in mats]
    row_no = lax.broadcasted_iota(jnp.int32, (8, 128), 0)
    both = range(len(mats))
    for step in range(first, last):
        cols = [[lanes(tiles[w][step], 8 * step + m) for m in range(8)] for w in both]
        below = [
            {i: [lanes(tiles[w][i], 8 * step + m) for m in range(8)] for i in range(step + 1, RANK // 8)} for w in both
        ]
        lower = [tiles[w][step] for w in both]
        solved = [tiles[w][step] for w in both]
        for i in range(8):
            for w in both:
                inv = 1.0 / subs(cols[w][i], i)
                pivot_row = subs(lower[w], i) * inv
                others = jnp.where(row_no != i, cols[w][i], 0.0)
                for m in range(i + 1, 8):
                    pivot = subs(cols[w][m], i) * inv
                    cols[w][m] = jnp.where(row_no == i, pivot, cols[w][m] - others * pivot)
                lower[w] = lower[w] - jnp.where(row_no > i, cols[w][i], 0.0) * pivot_row
                solved[w] = jnp.where(row_no == i, pivot_row, solved[w] - others * pivot_row)
        for w in both:
            tiles[w][step] = lower[w]
            rows = [subs(solved[w], m) for m in range(8)]
            for i in range(step + 1, RANK // 8):
                for m in range(8):
                    tiles[w][i] = tiles[w][i] - below[w][i][m] * rows[m]
    return [jnp.concatenate(t, axis=0) for t in tiles]


def kernel_gram(devices, last, *refs):
    s_ref, m_ref = refs[-2 - STREAMS : -STREAMS]
    mats = []
    eye = (
        lax.broadcasted_iota(jnp.int32, (RANK, RANK), 0) == lax.broadcasted_iota(jnp.int32, (RANK, RANK), 1)
    ).astype(F32)
    for which in range(2):
        for k in range(3):
            parts, rows = gather_parts(devices, which, refs[which * 2 * STREAMS :][: 2 * STREAMS], k)
            for part, row in zip(parts, rows):
                s_ref[which, k, pl.ds(row, PART)] = part
        gram = jnp.zeros((RANK, RANK), F32)
        for k in range(3):
            s = s_ref[which, k]
            gram += lax.dot_general(s, s, (((1,), (1,)), ((), ())), precision=HIGH, preferred_element_type=F32)
        mats.append(jnp.concatenate([gram * (1.0 / (3 * C)), eye], axis=1))
    mats = eliminate(mats, 0, last)
    for which in range(2):
        m_ref[which] = mats[which]
    clear(refs[-STREAMS:])


def gram(devices, last, parts, tie):
    return pl.pallas_call(
        functools.partial(kernel_gram, devices, last),
        out_shape=[
            pltpu.VMEM((LAYERS, 3, RANK, C), F32),
            pltpu.VMEM((LAYERS, RANK, 2 * RANK), F32),
        ]
        + TOKENS,
        in_specs=[spec(pltpu.VMEM)] * len(parts) + [spec(pl.ANY)],
        out_specs=[spec(pltpu.VMEM)] * (2 + STREAMS),
        compiler_params=pltpu.CompilerParams(vmem_limit_bytes=VMEM_LIMIT),
        cost_estimate=cost(2 * 10**9, 10 * 10**6),
        name="gram",
    )(*parts, tie)


def kernel_middle(first, last, m_ref, tie_ref, out_ref, *token_refs):
    mats = eliminate([m_ref[0], m_ref[1]], first, last)
    for which in range(2):
        out_ref[which] = mats[which]
    clear(token_refs)


def middle(first, last, m, tie):
    return pl.pallas_call(
        functools.partial(kernel_middle, first, last),
        out_shape=[pltpu.VMEM((LAYERS, RANK, 2 * RANK), F32)] + TOKENS,
        in_specs=[spec(pltpu.VMEM), spec(pl.ANY)],
        out_specs=[spec(pltpu.VMEM)] * (1 + STREAMS),
        compiler_params=pltpu.CompilerParams(vmem_limit_bytes=VMEM_LIMIT),
        cost_estimate=cost(2 * 10**9, 10 * 10**6),
        name=f"middle_{first}",
    )(local(m), tie)


def kernel_panels(first, s_ref, m_ref, tie_ref, inv_ref, p_ref, pp_ref, *token_refs):
    mats = eliminate([m_ref[0], m_ref[1]], first, RANK // 8)
    eye = (
        lax.broadcasted_iota(jnp.int32, (RANK, RANK), 0) == lax.broadcasted_iota(jnp.int32, (RANK, RANK), 1)
    ).astype(F32)
    for which in range(2):
        layer = place(which)
        m = mats[which]
        diag = jnp.sum(m[:, :RANK] * eye, axis=1, keepdims=True)
        inv = m[:, RANK:] * (1.0 / jnp.sqrt(diag))
        inv_ref[which] = inv
        for k in range(3):
            p_t = lax.dot_general(
                inv, s_ref[which, k], (((1,), (0,)), ((), ())), precision=HIGH, preferred_element_type=F32
            )
            p_ref[layer, :, pl.ds(k * C, C)] = p_t
            hi, lo = split2(p_t.T)
            pp_ref[which, pl.ds(k * C, C)] = jnp.concatenate([hi, lo, hi], axis=1)
    clear(token_refs)


def panels(first, s, m, tie):
    return pl.pallas_call(
        functools.partial(kernel_panels, first),
        out_shape=[
            pltpu.VMEM((LAYERS, RANK, RANK), F32),
            jax.ShapeDtypeStruct((LAYERS, RANK, 3 * C), F32),
            pltpu.VMEM((LAYERS, 3 * C, 3 * RANK), BF16),
        ]
        + TOKENS,
        in_specs=[spec(pltpu.VMEM), spec(pltpu.VMEM), spec(pl.ANY)],
        out_specs=[spec(pltpu.VMEM)] * (3 + STREAMS),
        compiler_params=pltpu.CompilerParams(vmem_limit_bytes=VMEM_LIMIT),
        cost_estimate=cost(2 * 10**9, 10 * 10**6),
        name="panels",
    )(local(s), local(m), tie)


def layer_error(devices, which, f_refs, inv_ref, pp_ref, g_refs, err_ref, first, each):
    norm = 1.0 / math.sqrt(3 * C * devices)
    f = jnp.concatenate([f_ref[...] for f_ref in f_refs], axis=0)
    f_t = (
        lax.dot_general(
            inv_ref[which], f, (((1,), (0,)), ((), ())), precision=HIGH, preferred_element_type=F32
        )
        * norm
    )
    first(f_t)
    hi, lo = split2(f_t * norm)
    rhs = jnp.concatenate([hi, hi, lo], axis=0)
    for k in range(3):
        rows = pl.ds(k * C, C)
        err_ref[rows] = (g_refs[k][...] - dot_nn(pp_ref[which, rows], rhs)).astype(BF16)
        each(k)


def kernel_own_error(devices, *refs):
    f_refs, (inv_ref, pp_ref, g0, g1, g2, factor_ref, err_ref) = refs[:STREAMS], refs[STREAMS:]

    def keep_factor(f_t):
        factor_ref[...] = f_t

    layer_error(devices, 0, f_refs, inv_ref, pp_ref, (g0, g1, g2), err_ref, keep_factor, lambda k: None)


def kernel_errors(devices, *refs):
    f_refs, (inv_ref, pp_ref, g0, g1, g2, own_factor, own_err) = refs[:STREAMS], refs[STREAMS : STREAMS + 7]
    factor_hbm, err_hbm, err_ref, factor_ref, sems = refs[STREAMS + 7 :]
    copies = []

    def write(source, which, k):
        rows = pl.ds(k * C, C)
        copy = pltpu.make_async_copy(source.at[rows], err_hbm.at[place(which), rows], sems.at[which, k])
        copy.start()
        copies.append(copy)

    def write_factor(source, which):
        copy = pltpu.make_async_copy(source, factor_hbm.at[place(which)], sems.at[which, 3])
        copy.start()
        copies.append(copy)

    def keep_factor(f_t):
        factor_ref[...] = f_t
        write_factor(factor_ref, 1)

    for k in range(3):
        write(own_err, 0, k)
    write_factor(own_factor, 0)
    layer_error(devices, 1, f_refs, inv_ref, pp_ref, (g0, g1, g2), err_ref, keep_factor, lambda k: write(err_ref, 1, k))
    for copy in copies:
        copy.wait()


def own_error(devices, f, inv, pp, blocks):
    return pl.pallas_call(
        functools.partial(kernel_own_error, devices),
        out_shape=[pltpu.VMEM((RANK, C), F32), pltpu.VMEM((3 * C, C), BF16)],
        in_specs=[spec(pltpu.VMEM)] * (5 + STREAMS),
        out_specs=[spec(pltpu.VMEM)] * 2,
        compiler_params=pltpu.CompilerParams(vmem_limit_bytes=VMEM_LIMIT),
        cost_estimate=cost(10**9, 5 * 10**6),
        name="own_error",
    )(*f, local(inv), local(pp), *[local(blocks[0, k][0]) for k in range(3)])


def errors(devices, f, inv, pp, blocks, own_factor, own_err):
    return pl.pallas_call(
        functools.partial(kernel_errors, devices),
        out_shape=[pltpu.HBM((LAYERS, RANK, C), F32), pltpu.HBM((LAYERS, 3 * C, C), BF16)],
        in_specs=[spec(pltpu.VMEM)] * (7 + STREAMS),
        out_specs=[spec(pltpu.HBM)] * 2,
        scratch_shapes=[
            pltpu.VMEM((3 * C, C), BF16),
            pltpu.VMEM((RANK, C), F32),
            pltpu.SemaphoreType.DMA((2, 4)),
        ],
        compiler_params=pltpu.CompilerParams(vmem_limit_bytes=VMEM_LIMIT),
        cost_estimate=cost(10**9, 5 * 10**6),
        name="errors",
    )(*f, local(inv), local(pp), *[local(blocks[1, k][0]) for k in range(3)], local(own_factor), local(own_err))


def body(devices, x, o, e, q):
    orders = exchange_bits(devices)
    steps = len(orders[0])

    def swap_core(v):
        return lax.ppermute(v, "dp", [(i, i ^ 1) for i in range(devices)])

    def added(held, arrived, tokens):
        return [v + w + token for v, w, token in zip(held, arrived, tokens)]

    def added_in_turn(held, arrived, tokens):
        total = list(held)
        for i in reversed(range(STREAMS)):
            token = tokens[i] if i == STREAMS - 1 else gate([tokens[i]], total[i + 1])[0]
            total[i] = held[i] + (arrived[i] + token)
        return total

    def swap(v, step):
        return lax.ppermute(v, "dp", [(i, i ^ (1 << orders[i & 1][step])) for i in range(devices)])

    q = jnp.swapaxes(q, 1, 2)
    other, x1, o1, e1, x0, o0, e0, q_all = load(devices, x, o, e, q)
    got = swap_core(other)
    own = sums(devices, q_all, x0, o0, e0)
    sent = [own[0, i] + got[0, i] for i in range(STREAMS)]
    held = [own[1, i] + got[1, i] for i in range(STREAMS)]
    arrays = ((x0, o0, e0), (x1, o1, e1))
    blocks = {}
    plan = PLAN if steps + 1 >= len(PLAN) else [sum(PLAN, ())]
    for step in range(steps + 1):
        if step == 0:
            arrived = [swap(v, 0) for v in sent]
        else:
            arrived = [swap(v, step % steps) for v in held]
        if step < len(plan) and plan[step]:
            formed, tokens = grads(plan[step], arrays, held[-1])
            blocks.update(formed)
        if step < steps:
            if step < len(plan) and plan[step]:
                held = added(held, arrived, tokens)
            else:
                held = [v + w for v, w in zip(held, arrived)]
    own_parts = [v for pair in zip(held, arrived) for v in pair]
    other_parts = [swap_core(v) for v in own_parts]
    f1 = right(devices, 1, other_parts, blocks)
    f0 = right(devices, 0, own_parts, blocks)
    f0 = [v + swap_core(w) for v, w in zip(f0, f1)]
    s_all, mat, *tokens = gram(devices, CUTS[0], own_parts + other_parts, f0[-1])
    for step in range(steps):
        arrived = [swap(v, step) for v in f0]
        if step == 1:
            mat, *tokens = middle(CUTS[0], CUTS[1], mat, f0[-1])
        if step == 2:
            inv, panel, pp, *tokens = panels(CUTS[1], s_all, mat, f0[-1])
        f0 = added_in_turn(f0, arrived, tokens) if step < 3 else [v + w for v, w in zip(f0, arrived)]
    f1 = [swap_core(v) for v in f0]
    own_factor, own_err = own_error(devices, f0, inv, pp, blocks)
    factors, error = errors(devices, f1, inv, pp, blocks, own_factor, own_err)
    return jnp.swapaxes(panel, 1, 2), jnp.swapaxes(factors, 1, 2), error


def solution(mesh):
    devices = mesh.shape["dp"]
    in_specs = (
        P(None, ("groups", "dp"), None, None),
        P(None, ("groups", "dp"), None, None),
        P(None, ("groups", "dp"), None),
        P(),
    )
    out_specs = (P("groups", None, None), P("groups", None, None), P(None, ("groups", "dp"), None))
    return jax.shard_map(
        functools.partial(body, devices), mesh=mesh, in_specs=in_specs, out_specs=out_specs, check_vma=False
    )
```

```python
import functools
import math

import jax
import jax.numpy as jnp
from jax import lax
from jax.experimental import pallas as pl
from jax.experimental.pallas import tpu as pltpu
from jax.sharding import PartitionSpec as P

C = 512
RANK = 64
LEN = 1344
LAYERS = 2
DILATION = 64
PAD = 64
STREAMS = 2
PART = RANK // (2 * STREAMS)
F32 = jnp.float32
BF16 = jnp.bfloat16
HIGH = lax.Precision.HIGHEST
VMEM_LIMIT = 14 << 20
CUTS = (3, 8)
PLAN = [((0, 0), (0, 1)), ((0, 2), (1, 0)), ((1, 1), (1, 2))]


def exchange_bits(devices):
    bits = list(range(1, devices.bit_length() - 1))
    return bits, bits[1:] + bits[:1]


def dot_nn(a, b):
    return lax.dot_general(a, b, (((1,), (0,)), ((), ())), preferred_element_type=F32)


def dot_nt(a, b):
    return lax.dot_general(a, b, (((1,), (1,)), ((), ())), preferred_element_type=F32)


def dot_tn(a, b):
    return lax.dot_general(a, b, (((0,), (0,)), ((), ())), preferred_element_type=F32)


def split2(v):
    hi = v.astype(BF16)
    return hi, (v - hi.astype(F32)).astype(BF16)


def place(which):
    core = lax.rem(lax.axis_index("dp"), 2)
    return core if which == 0 else 1 - core


def kept(devices, layer):
    orders = exchange_bits(devices)
    return (lax.axis_index("dp") >> jnp.where(layer == 0, orders[0][0], orders[1][0])) & 1


def spec(space):
    return pl.BlockSpec(memory_space=space)


def local(v):
    return pltpu.with_memory_space_constraint(v, pltpu.VMEM)


def far(v):
    return pltpu.with_memory_space_constraint(v, pltpu.HBM)


TOKENS = [pltpu.VMEM((2 * PART, C), F32)] * STREAMS


def clear(refs):
    for ref in refs:
        ref[...] = jnp.zeros_like(ref)


def cost(flops, nbytes):
    return pl.CostEstimate(flops=flops, transcendentals=0, bytes_accessed=nbytes)


def layer_sum(devices, layer, q_ref, x_ref, o_ref, e_ref, waits, out_ref):
    keep = kept(devices, layer)
    q_t = q_ref[layer] * (1.0 / math.sqrt(devices))
    q_hi = q_t.astype(BF16)
    q_mid, q_low = split2(q_t - q_hi.astype(F32))
    q_all = jnp.concatenate([q_hi, q_mid, q_low], axis=0)
    waits[0]()
    oq_all = dot_nt(q_all, o_ref[pl.ds(PAD, LEN + PAD)])
    oq = (oq_all[:RANK] + oq_all[RANK : 2 * RANK] + oq_all[2 * RANK :]) * (1.0 / math.sqrt(LEN))
    spacing = (DILATION // 2) * (1 + layer)
    width = LEN + PAD
    pieces = []
    for shifted in (pltpu.roll(oq, width - spacing, 1), oq, pltpu.roll(oq, spacing, 1)):
        pieces.extend(split2(shifted))
    lhs = jnp.concatenate(pieces, axis=0)
    waits[1]()
    prod = dot_nn(lhs, x_ref[...])
    waits[2]()
    for k in range(3):
        eq_all = dot_nt(q_all, e_ref[pl.ds(k * C, C)])
        eq = eq_all[:RANK] + eq_all[RANK : 2 * RANK] + eq_all[2 * RANK :]
        total = prod[k * 128 : k * 128 + RANK] + prod[k * 128 + RANK : k * 128 + 128] + eq
        for i in range(2 * STREAMS):
            slot = jnp.where(keep == i % 2, 1, 0)
            out_ref[slot, i // 2, k] = total[i * PART : (i + 1) * PART]


def kernel_load(devices, x_hbm, o_hbm, e_hbm, q_hbm, out_ref, x1, o1, e1, x0, o0, e0, q_ref, sems):
    copies = [pltpu.make_async_copy(q_hbm, q_ref, sems.at[2, 0])]
    for which, x_ref, o_ref, e_ref in ((1, x1, o1, e1), (0, x0, o0, e0)):
        layer = place(which)
        copies += [
            pltpu.make_async_copy(o_hbm.at[layer, 0], o_ref.at[pl.ds(PAD, LEN)], sems.at[which, 0]),
            pltpu.make_async_copy(x_hbm.at[layer, 0], x_ref.at[pl.ds(0, LEN)], sems.at[which, 1]),
            pltpu.make_async_copy(e_hbm.at[layer], e_ref, sems.at[which, 2]),
        ]
    for copy in copies:
        copy.start()
    zeros = jnp.zeros((PAD, C), BF16)
    for x_ref, o_ref in ((x1, o1), (x0, o0)):
        o_ref[pl.ds(0, PAD)] = zeros
        o_ref[pl.ds(PAD + LEN, PAD)] = zeros
        x_ref[pl.ds(LEN, PAD)] = zeros
    copies[0].wait()
    layer_sum(devices, place(1), q_ref, x1, o1, e1, [copy.wait for copy in copies[1:4]], out_ref)
    for copy in copies[4:]:
        copy.wait()


def load(devices, x, o, e, q):
    return pl.pallas_call(
        functools.partial(kernel_load, devices),
        out_shape=[
            pltpu.VMEM((2, STREAMS, 3, PART, C), F32),
            pltpu.VMEM((LEN + PAD, C), BF16),
            pltpu.VMEM((LEN + 2 * PAD, C), BF16),
            pltpu.VMEM((3 * C, C), BF16),
            pltpu.VMEM((LEN + PAD, C), BF16),
            pltpu.VMEM((LEN + 2 * PAD, C), BF16),
            pltpu.VMEM((3 * C, C), BF16),
            pltpu.VMEM((LAYERS, RANK, C), F32),
        ],
        in_specs=[spec(pltpu.HBM)] * 4,
        out_specs=[spec(pltpu.VMEM)] * 8,
        scratch_shapes=[pltpu.SemaphoreType.DMA((3, 3))],
        compiler_params=pltpu.CompilerParams(vmem_limit_bytes=VMEM_LIMIT),
        cost_estimate=cost(2 * 10**9, 9 * 10**6),
        name="load",
    )(far(x), far(o), far(e), far(q))


def kernel_sums(devices, q_ref, x_ref, o_ref, e_ref, out_ref):
    layer_sum(devices, place(0), q_ref, x_ref, o_ref, e_ref, [lambda: None] * 3, out_ref)


def sums(devices, q, x, o, e):
    return pl.pallas_call(
        functools.partial(kernel_sums, devices),
        out_shape=pltpu.VMEM((2, STREAMS, 3, PART, C), F32),
        in_specs=[spec(pltpu.VMEM)] * 4,
        out_specs=spec(pltpu.VMEM),
        compiler_params=pltpu.CompilerParams(vmem_limit_bytes=VMEM_LIMIT),
        cost_estimate=cost(2 * 10**9, 4 * 10**6),
        name="sums",
    )(local(q), local(x), local(o), local(e))


def kernel_grads(parts, *refs):
    ins, outs = refs[: 3 * len(parts)], refs[3 * len(parts) + 1 :]
    for i, (which, k) in enumerate(parts):
        x_ref, o_ref, e_ref = ins[3 * i : 3 * i + 3]
        g_ref, hi_ref, lo_ref = outs[3 * i : 3 * i + 3]
        spacing = (DILATION // 2) * (1 + place(which))
        start = pl.multiple_of(PAD - (k - 1) * spacing, 32)
        prod = dot_tn(x_ref[pl.ds(0, LEN)], o_ref[pl.ds(start, LEN)])
        g = prod * (1.0 / math.sqrt(LEN)) + e_ref[pl.ds(k * C, C)].astype(F32)
        g_ref[...] = g
        hi_ref[...], lo_ref[...] = split2(g)
    clear(outs[-STREAMS:])


def grads(parts, arrays, tie):
    ins = [local(v) for which, _ in parts for v in arrays[which]]
    block = [pltpu.VMEM((C, C), F32), pltpu.VMEM((C, C), BF16), pltpu.VMEM((C, C), BF16)]
    out = pl.pallas_call(
        functools.partial(kernel_grads, parts),
        out_shape=block * len(parts) + [pltpu.VMEM((3, PART, C), F32)] * STREAMS,
        in_specs=[spec(pltpu.VMEM)] * len(ins) + [spec(pl.ANY)],
        out_specs=[spec(pltpu.VMEM)] * (3 * len(parts) + STREAMS),
        compiler_params=pltpu.CompilerParams(vmem_limit_bytes=VMEM_LIMIT),
        cost_estimate=cost(10**9 * len(parts), 3 * 10**6 * len(parts)),
        name="grads_" + "_".join(f"{which}{k}" for which, k in parts),
    )(*ins, tie)
    return {part: out[3 * i : 3 * i + 3] for i, part in enumerate(parts)}, out[-STREAMS:]


def kernel_gate(*refs):
    pass


def gate(values, tie):
    n = len(values)
    return pl.pallas_call(
        kernel_gate,
        out_shape=[pltpu.VMEM(v.shape, v.dtype) for v in values],
        in_specs=[spec(pltpu.VMEM)] * n + [spec(pl.ANY)],
        out_specs=[spec(pltpu.VMEM)] * n,
        input_output_aliases={i: i for i in range(n)},
        compiler_params=pltpu.CompilerParams(vmem_limit_bytes=VMEM_LIMIT),
        cost_estimate=cost(0, 0),
        name="gate",
    )(*[local(v) for v in values], tie)


def gather_parts(devices, which, part_refs, k):
    keep = kept(devices, place(which))
    rows = [(2 * (i // 2) + (keep if i % 2 == 0 else 1 - keep)) * PART for i in range(len(part_refs))]
    return [ref[k] for ref in part_refs], [pl.multiple_of(row, PART) for row in rows]


def kernel_right(devices, which, *refs):
    part_refs, his, los, f_refs = refs[: 2 * STREAMS], refs[2 * STREAMS :][:3], refs[2 * STREAMS + 3 :][:3], refs[-STREAMS:]
    acc = jnp.zeros((2 * RANK, C), F32)
    acc_low = jnp.zeros((RANK, C), F32)
    for k in range(3):
        parts, rows = gather_parts(devices, which, part_refs, k)
        s_hi, s_lo = split2(jnp.concatenate(parts, axis=0))
        acc += dot_nn(jnp.concatenate([s_hi, s_lo], axis=0), his[k][...])
        acc_low += dot_nn(s_hi, los[k][...])
    f = acc[:RANK] + acc[RANK:] + acc_low
    for i, row in enumerate(rows):
        row = pl.multiple_of(row - (i // 2) * 2 * PART, PART)
        f_refs[i // 2][pl.ds(row, PART)] = f[i * PART : (i + 1) * PART]


def right(devices, which, parts, blocks):
    his = [local(blocks[which, k][1]) for k in range(3)]
    los = [local(blocks[which, k][2]) for k in range(3)]
    return pl.pallas_call(
        functools.partial(kernel_right, devices, which),
        out_shape=[pltpu.VMEM((2 * PART, C), F32)] * STREAMS,
        in_specs=[spec(pltpu.VMEM)] * (2 * STREAMS + 6),
        out_specs=[spec(pltpu.VMEM)] * STREAMS,
        compiler_params=pltpu.CompilerParams(vmem_limit_bytes=VMEM_LIMIT),
        cost_estimate=cost(10**9, 4 * 10**6),
        name=f"right_{which}",
    )(*parts, *his, *los)


def lanes(v, column):
    return jnp.broadcast_to(v[:, column : column + 1], (8, 128))


def subs(v, row):
    return jnp.broadcast_to(v[row : row + 1, :], (8, 128))


def eliminate(mats, first, last):
    tiles = [[m[8 * i : 8 * i + 8] for i in range(RANK // 8)] for m in mats]
    row_no = lax.broadcasted_iota(jnp.int32, (8, 128), 0)
    both = range(len(mats))
    for step in range(first, last):
        cols = [[lanes(tiles[w][step], 8 * step + m) for m in range(8)] for w in both]
        below = [
            {i: [lanes(tiles[w][i], 8 * step + m) for m in range(8)] for i in range(step + 1, RANK // 8)} for w in both
        ]
        lower = [tiles[w][step] for w in both]
        solved = [tiles[w][step] for w in both]
        for i in range(8):
            for w in both:
                inv = 1.0 / subs(cols[w][i], i)
                pivot_row = subs(lower[w], i) * inv
                others = jnp.where(row_no != i, cols[w][i], 0.0)
                for m in range(i + 1, 8):
                    pivot = subs(cols[w][m], i) * inv
                    cols[w][m] = jnp.where(row_no == i, pivot, cols[w][m] - others * pivot)
                lower[w] = lower[w] - jnp.where(row_no > i, cols[w][i], 0.0) * pivot_row
                solved[w] = jnp.where(row_no == i, pivot_row, solved[w] - others * pivot_row)
        for w in both:
            tiles[w][step] = lower[w]
            rows = [subs(solved[w], m) for m in range(8)]
            for i in range(step + 1, RANK // 8):
                for m in range(8):
                    tiles[w][i] = tiles[w][i] - below[w][i][m] * rows[m]
    return [jnp.concatenate(t, axis=0) for t in tiles]


def kernel_gram(devices, last, *refs):
    s_ref, m_ref = refs[-2 - STREAMS : -STREAMS]
    mats = []
    eye = (
        lax.broadcasted_iota(jnp.int32, (RANK, RANK), 0) == lax.broadcasted_iota(jnp.int32, (RANK, RANK), 1)
    ).astype(F32)
    for which in range(2):
        for k in range(3):
            parts, rows = gather_parts(devices, which, refs[which * 2 * STREAMS :][: 2 * STREAMS], k)
            for part, row in zip(parts, rows):
                s_ref[which, k, pl.ds(row, PART)] = part
        gram = jnp.zeros((RANK, RANK), F32)
        for k in range(3):
            s = s_ref[which, k]
            gram += lax.dot_general(s, s, (((1,), (1,)), ((), ())), precision=HIGH, preferred_element_type=F32)
        mats.append(jnp.concatenate([gram * (1.0 / (3 * C)), eye], axis=1))
    mats = eliminate(mats, 0, last)
    for which in range(2):
        m_ref[which] = mats[which]
    clear(refs[-STREAMS:])


def gram(devices, last, parts, tie):
    return pl.pallas_call(
        functools.partial(kernel_gram, devices, last),
        out_shape=[
            pltpu.VMEM((LAYERS, 3, RANK, C), F32),
            pltpu.VMEM((LAYERS, RANK, 2 * RANK), F32),
        ]
        + TOKENS,
        in_specs=[spec(pltpu.VMEM)] * len(parts) + [spec(pl.ANY)],
        out_specs=[spec(pltpu.VMEM)] * (2 + STREAMS),
        compiler_params=pltpu.CompilerParams(vmem_limit_bytes=VMEM_LIMIT),
        cost_estimate=cost(2 * 10**9, 10 * 10**6),
        name="gram",
    )(*parts, tie)


def kernel_middle(first, last, m_ref, tie_ref, out_ref, *token_refs):
    mats = eliminate([m_ref[0], m_ref[1]], first, last)
    for which in range(2):
        out_ref[which] = mats[which]
    clear(token_refs)


def middle(first, last, m, tie):
    return pl.pallas_call(
        functools.partial(kernel_middle, first, last),
        out_shape=[pltpu.VMEM((LAYERS, RANK, 2 * RANK), F32)] + TOKENS,
        in_specs=[spec(pltpu.VMEM), spec(pl.ANY)],
        out_specs=[spec(pltpu.VMEM)] * (1 + STREAMS),
        compiler_params=pltpu.CompilerParams(vmem_limit_bytes=VMEM_LIMIT),
        cost_estimate=cost(2 * 10**9, 10 * 10**6),
        name=f"middle_{first}",
    )(local(m), tie)


def kernel_panels(first, s_ref, m_ref, tie_ref, inv_ref, p_ref, pp_ref, *token_refs):
    mats = eliminate([m_ref[0], m_ref[1]], first, RANK // 8)
    eye = (
        lax.broadcasted_iota(jnp.int32, (RANK, RANK), 0) == lax.broadcasted_iota(jnp.int32, (RANK, RANK), 1)
    ).astype(F32)
    for which in range(2):
        layer = place(which)
        m = mats[which]
        diag = jnp.sum(m[:, :RANK] * eye, axis=1, keepdims=True)
        inv = m[:, RANK:] * (1.0 / jnp.sqrt(diag))
        inv_ref[which] = inv
        for k in range(3):
            p_t = lax.dot_general(
                inv, s_ref[which, k], (((1,), (0,)), ((), ())), precision=HIGH, preferred_element_type=F32
            )
            p_ref[layer, :, pl.ds(k * C, C)] = p_t
            hi, lo = split2(p_t.T)
            pp_ref[which, pl.ds(k * C, C)] = jnp.concatenate([hi, lo, hi], axis=1)
    clear(token_refs)


def panels(first, s, m, tie):
    return pl.pallas_call(
        functools.partial(kernel_panels, first),
        out_shape=[
            pltpu.VMEM((LAYERS, RANK, RANK), F32),
            pltpu.VMEM((LAYERS, RANK, 3 * C), F32),
            pltpu.VMEM((LAYERS, 3 * C, 3 * RANK), BF16),
        ]
        + TOKENS,
        in_specs=[spec(pltpu.VMEM), spec(pltpu.VMEM), spec(pl.ANY)],
        out_specs=[spec(pltpu.VMEM)] * (3 + STREAMS),
        compiler_params=pltpu.CompilerParams(vmem_limit_bytes=VMEM_LIMIT),
        cost_estimate=cost(2 * 10**9, 10 * 10**6),
        name="panels",
    )(local(s), local(m), tie)


def layer_error(devices, which, f_refs, inv_ref, pp_ref, g_refs, err_ref, first, each):
    norm = 1.0 / math.sqrt(3 * C * devices)
    f = jnp.concatenate([f_ref[...] for f_ref in f_refs], axis=0)
    f_t = (
        lax.dot_general(
            inv_ref[which], f, (((1,), (0,)), ((), ())), precision=HIGH, preferred_element_type=F32
        )
        * norm
    )
    first(f_t)
    hi, lo = split2(f_t * norm)
    rhs = jnp.concatenate([hi, hi, lo], axis=0)
    for k in range(3):
        rows = pl.ds(k * C, C)
        err_ref[rows] = (g_refs[k][...] - dot_nn(pp_ref[which, rows], rhs)).astype(BF16)
        each(k)


def kernel_own_error(devices, *refs):
    f_refs, (inv_ref, pp_ref, g0, g1, g2, p_ref) = refs[:STREAMS], refs[STREAMS : STREAMS + 6]
    factor_ref, err_ref, p_hbm, sem = refs[STREAMS + 6 :]
    copy = pltpu.make_async_copy(p_ref, p_hbm, sem)
    copy.start()

    def keep_factor(f_t):
        factor_ref[...] = f_t

    layer_error(devices, 0, f_refs, inv_ref, pp_ref, (g0, g1, g2), err_ref, keep_factor, lambda k: None)
    copy.wait()


def kernel_errors(devices, *refs):
    f_refs, (inv_ref, pp_ref, g0, g1, g2, own_factor, own_err) = refs[:STREAMS], refs[STREAMS : STREAMS + 7]
    factor_hbm, err_hbm, err_ref, factor_ref, sems = refs[STREAMS + 7 :]
    copies = []

    def write(source, which, k):
        rows = pl.ds(k * C, C)
        copy = pltpu.make_async_copy(source.at[rows], err_hbm.at[place(which), rows], sems.at[which, k])
        copy.start()
        copies.append(copy)

    def write_factor(source, which):
        copy = pltpu.make_async_copy(source, factor_hbm.at[place(which)], sems.at[which, 3])
        copy.start()
        copies.append(copy)

    def keep_factor(f_t):
        factor_ref[...] = f_t
        write_factor(factor_ref, 1)

    for k in range(3):
        write(own_err, 0, k)
    write_factor(own_factor, 0)
    layer_error(devices, 1, f_refs, inv_ref, pp_ref, (g0, g1, g2), err_ref, keep_factor, lambda k: write(err_ref, 1, k))
    for copy in copies:
        copy.wait()


def own_error(devices, f, inv, pp, blocks, panel):
    return pl.pallas_call(
        functools.partial(kernel_own_error, devices),
        out_shape=[pltpu.VMEM((RANK, C), F32), pltpu.VMEM((3 * C, C), BF16), pltpu.HBM(panel.shape, F32)],
        in_specs=[spec(pltpu.VMEM)] * (6 + STREAMS),
        out_specs=[spec(pltpu.VMEM)] * 2 + [spec(pltpu.HBM)],
        scratch_shapes=[pltpu.SemaphoreType.DMA],
        compiler_params=pltpu.CompilerParams(vmem_limit_bytes=VMEM_LIMIT),
        cost_estimate=cost(10**9, 5 * 10**6),
        name="own_error",
    )(*f, local(inv), local(pp), *[local(blocks[0, k][0]) for k in range(3)], local(panel))


def errors(devices, f, inv, pp, blocks, own_factor, own_err):
    return pl.pallas_call(
        functools.partial(kernel_errors, devices),
        out_shape=[pltpu.HBM((LAYERS, RANK, C), F32), pltpu.HBM((LAYERS, 3 * C, C), BF16)],
        in_specs=[spec(pltpu.VMEM)] * (7 + STREAMS),
        out_specs=[spec(pltpu.HBM)] * 2,
        scratch_shapes=[
            pltpu.VMEM((3 * C, C), BF16),
            pltpu.VMEM((RANK, C), F32),
            pltpu.SemaphoreType.DMA((2, 4)),
        ],
        compiler_params=pltpu.CompilerParams(vmem_limit_bytes=VMEM_LIMIT),
        cost_estimate=cost(10**9, 5 * 10**6),
        name="errors",
    )(*f, local(inv), local(pp), *[local(blocks[1, k][0]) for k in range(3)], local(own_factor), local(own_err))


def body(devices, x, o, e, q):
    orders = exchange_bits(devices)
    steps = len(orders[0])

    def swap_core(v):
        return lax.ppermute(v, "dp", [(i, i ^ 1) for i in range(devices)])

    def added(held, arrived, tokens):
        return [v + w + token for v, w, token in zip(held, arrived, tokens)]

    def added_in_turn(held, arrived, tokens):
        total = list(held)
        for i in range(STREAMS):
            token = tokens[i] if i == 0 else gate([tokens[i]], total[i - 1])[0]
            total[i] = held[i] + (arrived[i] + token)
        return total

    def swap(v, step):
        return lax.ppermute(v, "dp", [(i, i ^ (1 << orders[i & 1][step])) for i in range(devices)])

    q = jnp.swapaxes(q, 1, 2)
    other, x1, o1, e1, x0, o0, e0, q_all = load(devices, x, o, e, q)
    got = swap_core(other)
    own = sums(devices, q_all, x0, o0, e0)
    sent = [own[0, i] + got[0, i] for i in range(STREAMS)]
    held = [own[1, i] + got[1, i] for i in range(STREAMS)]
    arrays = ((x0, o0, e0), (x1, o1, e1))
    blocks = {}
    plan = PLAN if steps + 1 >= len(PLAN) else [sum(PLAN, ())]
    for step in range(steps + 1):
        if step == 0:
            arrived = [swap(v, 0) for v in sent]
        else:
            arrived = [swap(v, step % steps) for v in held]
        if step < len(plan) and plan[step]:
            formed, tokens = grads(plan[step], arrays, held[-1])
            blocks.update(formed)
        if step < steps:
            if step < len(plan) and plan[step]:
                held = added(held, arrived, tokens)
            else:
                held = [v + w for v, w in zip(held, arrived)]
    own_parts = [v for pair in zip(held, arrived) for v in pair]
    other_parts = [swap_core(v) for v in own_parts]
    f1 = right(devices, 1, other_parts, blocks)
    f0 = right(devices, 0, own_parts, blocks)
    f0 = [v + swap_core(w) for v, w in zip(f0, f1)]
    s_all, mat, *tokens = gram(devices, CUTS[0], own_parts + other_parts, f0[-1])
    for step in range(steps):
        arrived = [swap(v, step) for v in f0]
        if step == 1:
            mat, *tokens = middle(CUTS[0], CUTS[1], mat, f0[-1])
        if step == 2:
            inv, panel, pp, *tokens = panels(CUTS[1], s_all, mat, f0[-1])
        f0 = added_in_turn(f0, arrived, tokens) if step < 3 else [v + w for v, w in zip(f0, arrived)]
    f1 = [swap_core(v) for v in f0]
    own_factor, own_err, panel = own_error(devices, f0, inv, pp, blocks, panel)
    factors, error = errors(devices, f1, inv, pp, blocks, own_factor, own_err)
    return jnp.swapaxes(panel, 1, 2), jnp.swapaxes(factors, 1, 2), error


def solution(mesh):
    devices = mesh.shape["dp"]
    in_specs = (
        P(None, ("groups", "dp"), None, None),
        P(None, ("groups", "dp"), None, None),
        P(None, ("groups", "dp"), None),
        P(),
    )
    out_specs = (P("groups", None, None), P("groups", None, None), P(None, ("groups", "dp"), None))
    return jax.shard_map(
        functools.partial(body, devices), mesh=mesh, in_specs=in_specs, out_specs=out_specs, check_vma=False
    )
```
